32 devices in a mesh: groups: 2 (over x), hits: 8 (over z, y), heads: 2 (over core).
Axes of the slice: x: 2, y: 2, z: 4, core: 2. Of those that a mesh axis runs over, the one named last changes fastest.
Arguments:
- queries: bfloat16 [2048, 2048], P('groups', 'heads'), parts along dimension 0, may hold values from -13.5 to 13.5
- keys: bfloat16 [8192, 2048], P(('groups', 'hits'), 'heads'), parts along dimension 0, may hold values from -36 to 36
- values: bfloat16 [8192, 2048], P(('groups', 'hits'), 'heads'), parts along dimension 0, may hold values from -6 to 6
- hit_counts: int32 [16], P(('groups', 'hits')), parts along dimension 0, may hold values from 128 to 512, as said below
- latents: bfloat16 [2048, 2048], P(('groups', 'hits'), 'heads'), parts along dimension 0, may hold values from -23 to 23
- out_proj: bfloat16 [2048, 2048], P('heads'), may hold values from -1 to 1
- norm_gain: float32 [2048], P('heads'), may hold values from 0.1 to 1.9
- up_proj: bfloat16 [2048, 8192], P('heads', 'hits'), may hold values from -0.125 to 0.125
- down_proj: bfloat16 [8192, 2048], P('hits', 'heads'), may hold values from -0.25 to 0.25
Outputs:
- mixed: bfloat16 [2048, 2048], P(('groups', 'hits'), 'heads'), parts along dimension 0
The draws below stay inside these ranges and needn't reach their ends.
There are 2 independent parts, one for each index of `groups`. The reference program is written for one: setup_inputs(seed, part) draws one part's arguments, and reference() takes and returns one part's arrays. A program takes and returns all parts, laid end to end along the dimension named above; an argument that names none is the same for every part. Nothing has to cross between parts.
Inputs may be any that keep to these rules, and one draw needn't show every extreme that they name: hit_counts[s] live hits fill the first slots of shard s; some shard is full and some holds exactly 128.
All inputs are finite; a program needn't handle non-finite values.
Results may differ from the reference program's by a relative error of at most 0.012.
Values may be sent and summed in bfloat16 or wider, within the bound.
No kernel may reach another device: no remote copies, remote signals or barrier semaphores. Data moves between devices by JAX's collectives and lax.ppermute only.
A program may use at most 64 MiB of HBM per device.

```python
import math
import jax
import jax.numpy as jnp
from jax import lax

L = 1024
D = 2048
NH = 16
HD = 128
F = 8192
HIT_DEV = 512
HITS = 4096
SHARDS = 8


def shared_draw(key):
    queries = 2.0 * jnp.clip(jax.random.normal(jax.random.fold_in(key, 11), (L, NH * HD), jnp.float32), -4.5, 4.5)
    keys = jnp.clip(jax.random.normal(jax.random.fold_in(key, 12), (HITS, NH * HD), jnp.float32), -4.5, 4.5)
    return (queries, keys)


def draw_queries(key, part):
    return shared_draw(key)[0].astype(jnp.bfloat16)


def draw_keys(key, part):
    return shared_draw(key)[1].astype(jnp.bfloat16)


def draw_hit_counts(key, part):
    counts = jax.random.randint(jax.random.fold_in(key, 21), (SHARDS,), HIT_DEV // 4, HIT_DEV + 1)
    order = jax.random.permutation(jax.random.fold_in(key, 22), SHARDS)
    counts = counts.at[order[0]].set(HIT_DEV)
    counts = counts.at[order[1]].set(HIT_DEV // 4)
    return counts.astype(jnp.int32)


def draw_latents(key, part):
    ramp = 0.2 * 10.0 ** (jnp.arange(D, dtype=jnp.float32) / (D - 1))
    jitter = jnp.exp(jax.random.uniform(jax.random.fold_in(key, 31), (D,), jnp.float32, jnp.log(0.7), jnp.log(1.4)))
    entries = jnp.clip(jax.random.normal(jax.random.fold_in(key, 32), (L, D), jnp.float32), -4.0, 4.0)
    row_scale = jnp.exp(jax.random.uniform(jax.random.fold_in(key, 33), (L,), jnp.float32, jnp.log(0.5), jnp.log(2.0)))
    return (entries * row_scale[:, None] * (ramp * jitter)[None, :]).astype(jnp.bfloat16)


def shard_levels(own_key, dims, pieces, smallest, top_value):
    def one(axis_at, shards_of):
        steps = jax.random.uniform(jax.random.fold_in(jax.random.fold_in(own_key, 6), axis_at), (shards_of,), jnp.float32, smallest / len(pieces), top_value / len(pieces))
        return jnp.repeat(jnp.exp(steps), dims[axis_at] // shards_of).reshape((-1,) + (1,) * (len(dims) - axis_at - 1))

    loudness = one(*pieces[0])
    for cut in pieces[1:]:
        loudness = loudness * one(*cut)
    return loudness


def centred(key, dims, width, bound, split=(), held_as=jnp.bfloat16):
    drawn = jax.random.normal(key, dims, jnp.float32) * width
    if len(split) > 0:
        drawn = shard_levels(key, dims, split, -0.22, 0.18) * drawn
    return jnp.clip(drawn, min=-bound, max=bound).astype(held_as)


def setup_inputs(seed: int = 0, part: int = 0) -> dict:
    key_of = jax.random.split(jax.random.key(seed), 10)
    own_keys = jax.random.split(jax.random.fold_in(key_of[9], part), 10)
    queries = draw_queries(jax.random.fold_in(jax.random.fold_in(key_of[9], part), 71), part)
    keys = draw_keys(jax.random.fold_in(jax.random.fold_in(key_of[9], part), 71), part)
    values = centred(own_keys[2], (HITS, NH * HD), 1.0, 6.0, ((0, 8), (1, 2)))
    hit_counts = draw_hit_counts(jax.random.fold_in(jax.random.fold_in(key_of[9], part), 71), part)
    latents = draw_latents(jax.random.fold_in(jax.random.fold_in(key_of[9], part), 71), part)
    out_proj = centred(key_of[5], (NH * HD, D), (max(D // 64, 8)) ** -0.5, 1.0, ((0, 2),))
    norm_gain = jnp.clip(1.0 + 0.18 * jax.random.normal(key_of[6], (D,), jnp.float32), 0.1, 1.9)
    up_proj = centred(key_of[7], (D, F), D ** -0.5, 0.125, ((0, 2), (1, 8)))
    down_proj = centred(key_of[8], (F, D), (max(F // 16, 8)) ** -0.5, 0.25, ((0, 8), (1, 2)))
    return dict(queries=queries, keys=keys, values=values, hit_counts=hit_counts, latents=latents, out_proj=out_proj, norm_gain=norm_gain, up_proj=up_proj, down_proj=down_proj)


def reference(queries, keys, values, hit_counts, latents, out_proj, norm_gain, up_proj, down_proj):
    positions = jnp.arange(HITS, dtype=jnp.int32)
    valid_hits = positions % HIT_DEV < hit_counts[positions // HIT_DEV]
    score_scale = 1.0 / math.sqrt(HD)

    def one_head(head_index):
        col_start = (head_index * HD).astype(jnp.int32)
        q_head = lax.dynamic_slice_in_dim(queries, col_start, HD, 1)
        k_head = lax.dynamic_slice_in_dim(keys, col_start, HD, 1)
        v_head = lax.dynamic_slice_in_dim(values, col_start, HD, 1)
        scores = lax.dot_general(q_head, k_head, (((1,), (1,)), ((), ())), preferred_element_type=jnp.float32) * score_scale
        scores = jnp.where(valid_hits[None, :], scores, -1e+30)
        row_top = lax.optimization_barrier(jnp.max(scores, axis=1))
        weights = jnp.where(valid_hits[None, :], jnp.exp(scores - row_top[:, None]), 0.0)
        row_total = lax.optimization_barrier(jnp.sum(weights, axis=1))
        context = jnp.dot(weights.astype(jnp.bfloat16), v_head, preferred_element_type=jnp.float32) / row_total[:, None]
        return context.astype(jnp.bfloat16)
    heads_out = lax.map(one_head, jnp.arange(NH, dtype=jnp.int32))
    context = heads_out.transpose(1, 0, 2).reshape(L, NH * HD)
    stream = latents.astype(jnp.float32) + jnp.dot(context, out_proj, preferred_element_type=jnp.float32)
    mean_square = lax.optimization_barrier(jnp.mean(stream * stream, axis=1))
    normed = (stream * lax.rsqrt(mean_square + 1e-06)[:, None] * norm_gain[None, :]).astype(jnp.bfloat16)
    hidden = jax.nn.gelu(jnp.dot(normed, up_proj, preferred_element_type=jnp.float32)).astype(jnp.bfloat16)
    mixed = stream + jnp.dot(hidden, down_proj, preferred_element_type=jnp.float32)
    return mixed.astype(jnp.bfloat16)
```

```python
import functools
import math

import jax
import jax.numpy as jnp
from jax import lax
from jax.experimental import pallas as pl
from jax.experimental.pallas import tpu as pltpu
from jax.sharding import PartitionSpec as P

HD = 128
BF = jnp.bfloat16
F32 = jnp.float32
EXP_SCALE = math.log2(math.e) / math.sqrt(HD)
DEAD = -1e30


def attn_kernel(heads, blocks, idx_ref, cnt_ref, *refs):
    q_refs, (k_ref, v_ref, ctx_ref, st_ref) = refs[:blocks], refs[blocks:]
    hits = k_ref.shape[0]
    live = lax.broadcasted_iota(jnp.int32, (hits, 1), 0) < cnt_ref[0]
    tops, sums = [], []
    for h in range(heads):
        cols = slice(h * HD, (h + 1) * HD)
        qh = q_refs[0][:, cols]
        if blocks > 1:
            qh = jnp.concatenate([r[:, cols] for r in q_refs], axis=0)
        s = lax.dot_general(k_ref[:, cols], qh, (((1,), (1,)), ((), ())), preferred_element_type=F32)
        s = jnp.where(live, s, DEAD)
        top = jnp.max(s, axis=0, keepdims=True).astype(BF).astype(F32)
        p = jnp.exp2((s - top) * EXP_SCALE)
        tops.append(top)
        sums.append(jnp.sum(p, axis=0, keepdims=True))
        ctx_ref[cols, :] = lax.dot_general(
            v_ref[:, cols], p.astype(BF), (((0,), (0,)), ((), ())), preferred_element_type=F32
        )
    st_ref[...] = jnp.concatenate(tops + sums, axis=0)


def attend(idx, cnt, q, k, v, rows):
    blocks = idx.shape[0]
    width, hits = k.shape[1], k.shape[0]
    heads = width // HD
    n = blocks * rows

    def q_spec(b):
        return pl.BlockSpec((rows, width), lambda i, idx_r, cnt_r: (idx_r[b], 0))

    whole = lambda shape: pl.BlockSpec(shape, lambda i, idx_r, cnt_r: (0, 0))
    return pl.pallas_call(
        functools.partial(attn_kernel, heads, blocks),
        grid_spec=pltpu.PrefetchScalarGridSpec(
            num_scalar_prefetch=2,
            grid=(1,),
            in_specs=[q_spec(b) for b in range(blocks)] + [whole(k.shape), whole(v.shape)],
            out_specs=[whole((width, n)), whole((2 * heads, n))],
        ),
        out_shape=[
            jax.ShapeDtypeStruct((width, n), F32),
            jax.ShapeDtypeStruct((2 * heads, n), F32),
        ],
        cost_estimate=pl.CostEstimate(
            flops=4 * n * hits * width,
            bytes_accessed=2 * k.size * 2 + n * width * 6,
            transcendentals=n * hits * heads,
        ),
        name="attend",
    )(idx, cnt, *([q] * blocks), k, v)


def group_rows(gh):
    return gh * HD + 4 * gh


def read_group(msg_ref, base, gh):
    st = msg_ref[base + gh * HD : base + gh * HD + 4 * gh, :].astype(F32)
    return st[:gh], st[gh : 2 * gh] + st[2 * gh : 3 * gh]


def write_stats(out_ref, base, gh, top, total):
    hi = total.astype(BF).astype(F32)
    st = jnp.concatenate([top, hi, total - hi, jnp.zeros_like(top)], axis=0)
    out_ref[base + gh * HD : base + gh * HD + 4 * gh, :] = st.astype(BF)


def merge_kernel(heads, jobs, lo, rows, *refs):
    gh = heads // 2
    gr = group_rows(gh)
    ctx_ref, st_ref = refs[0], refs[1]
    n_msg = sum(1 for j in jobs if j[2])
    msgs, outs = refs[2 : 2 + n_msg], refs[2 + n_msg :]
    at = 0
    for (b, groups, held), out_ref in zip(jobs, outs):
        cols = slice(b * rows, (b + 1) * rows)
        msg_ref = None
        if held:
            msg_ref = msgs[at]
            at += 1
        for g in groups:
            base = groups.index(g) * gr
            top = st_ref[g * gh : (g + 1) * gh, cols]
            total = st_ref[heads + g * gh : heads + (g + 1) * gh, cols]
            if g in held:
                mbase = held.index(g) * gr
                mtop, mtotal = read_group(msg_ref, mbase, gh)
                best = jnp.maximum(top, mtop)
                fa = jnp.exp2((top - best) * EXP_SCALE)
                fb = jnp.exp2((mtop - best) * EXP_SCALE)
                for h in range(gh):
                    src = slice((g * gh + h) * HD, (g * gh + h + 1) * HD)
                    mrc = slice(mbase + h * HD, mbase + (h + 1) * HD)
                    out_ref[base + h * HD : base + (h + 1) * HD, :] = (
                        ctx_ref[src, cols] * fa[h : h + 1]
                        + msg_ref[mrc, :].astype(F32) * fb[h : h + 1]
                    ).astype(BF)
                write_stats(out_ref, base, gh, best, total * fa + mtotal * fb)
            else:
                src = slice(g * gh * HD, (g + 1) * gh * HD)
                out_ref[base : base + gh * HD, :] = ctx_ref[src, cols].astype(BF)
                write_stats(out_ref, base, gh, top, total)


def merge(ctx, st, msgs, jobs, heads, rows):
    gr = group_rows(heads // 2)
    outs = [jax.ShapeDtypeStruct((len(j[1]) * gr, rows), BF) for j in jobs]
    nbytes = sum(len(j[1]) * gr * rows * 8 for j in jobs)
    return pl.pallas_call(
        functools.partial(merge_kernel, heads, jobs, 0, rows),
        out_shape=outs,
        cost_estimate=pl.CostEstimate(flops=nbytes, bytes_accessed=nbytes, transcendentals=0),
        name="merge",
    )(ctx, st, *msgs)


def finish_kernel(heads, rows, ctx_ref, st_ref, a_ref, b_ref, out_ref):
    gh = heads // 2
    gr = group_rows(gh)
    for g in range(2):
        top = st_ref[g * gh : (g + 1) * gh, :]
        total = st_ref[heads + g * gh : heads + (g + 1) * gh, :]
        atop, atotal = read_group(a_ref, g * gr, gh)
        btop, btotal = read_group(b_ref, g * gr, gh)
        best = jnp.maximum(jnp.maximum(top, atop), btop)
        f0 = jnp.exp2((top - best) * EXP_SCALE)
        fa = jnp.exp2((atop - best) * EXP_SCALE)
        fb = jnp.exp2((btop - best) * EXP_SCALE)
        total = total * f0 + atotal * fa + btotal * fb
        f0, fa, fb = f0 / total, fa / total, fb / total
        for h in range(gh):
            src = slice((g * gh + h) * HD, (g * gh + h + 1) * HD)
            mrc = slice(g * gr + h * HD, g * gr + (h + 1) * HD)
            c = (
                ctx_ref[src, :] * f0[h : h + 1]
                + a_ref[mrc, :].astype(F32) * fa[h : h + 1]
                + b_ref[mrc, :].astype(F32) * fb[h : h + 1]
            )
            out_ref[:, src] = jnp.transpose(c).astype(BF)


def finish(ctx, st, a, b, heads, rows):
    return pl.pallas_call(
        functools.partial(finish_kernel, heads, rows),
        out_shape=jax.ShapeDtypeStruct((rows, heads * HD), BF),
        cost_estimate=pl.CostEstimate(
            flops=rows * heads * HD * 8, bytes_accessed=rows * heads * HD * 10, transcendentals=0
        ),
        name="finish",
    )(ctx, st, a, b)


def make_shards(n):
    half = n // 2
    order = list(range(0, n, 2)) + list(range(n - 1, 0, -2))
    fwd = [(order[i], order[(i + 1) % n]) for i in range(n)]
    bwd = [(b, a) for a, b in fwd]
    swap = [(0, 1), (1, 0)]

    right = lambda x: lax.ppermute(x, "hits", fwd)
    left = lambda x: lax.ppermute(x, "hits", bwd)
    partner = lambda x: lax.ppermute(x, "heads", swap)

    def shards(queries, keys, values, hit_counts, latents, out_proj, norm_gain, up_proj, down_proj):
        core = lax.axis_index("heads")
        me = lax.axis_index("hits")
        pos = jnp.where(me % 2 == 0, me // 2, n - 1 - me // 2)

        def block_at(k):
            p = lax.rem(pos + (k + n), n)
            return jnp.where(p < half, 2 * p, 2 * (n - 1 - p) + 1)

        rows = latents.shape[0]
        mine = rows // 2
        width = keys.shape[1]
        heads = width // HD
        feats = 2 * latents.shape[1]
        fh = latents.shape[1]
        cnt = hit_counts.astype(jnp.int32)

        up_oth = partner(up_proj)
        down_oth = partner(down_proj)
        gain_oth = partner(norm_gain.reshape(1, fh))
        gain = jnp.concatenate([norm_gain.reshape(1, fh), gain_oth], axis=1)
        lat_mine = lax.dynamic_slice_in_dim(latents, core * mine, mine, 0)
        lat_oth = partner(lax.dynamic_slice_in_dim(latents, (1 - core) * mine, mine, 0))
        lat = jnp.concatenate([lat_mine, lat_oth], axis=1).astype(F32)

        def partial(ks):
            idx = jnp.stack([block_at(k) for k in ks]).astype(jnp.int32)
            return attend(idx, cnt, queries, keys, values, rows)

        ctx, st = partial([half])
        msg_r, msg_l = merge(ctx, st, [], ((0, (0,), ()), (0, (1,), ())), heads, rows)
        held_r, held_l = (0,), (1,)
        for t in range(2, half + 1):
            msg_r, msg_l = right(msg_r), left(msg_l)
            ctx, st = partial([half - t + 1, t - 1 - half])
            msg_r, msg_l = merge(
                ctx, st, [msg_r, msg_l], ((0, (0, 1), held_r), (1, (0, 1), held_l)), heads, rows
            )
            held_r = held_l = (0, 1)
        msg_r, msg_l = right(msg_r), left(msg_l)
        ctx, st = partial([0])
        context = finish(ctx, st, msg_r, msg_l, heads, rows)

        proj = jnp.dot(context, out_proj, preferred_element_type=F32)

        def own_first(x):
            a, b = x[:, :fh], x[:, fh:]
            return jnp.concatenate([jnp.where(core == 0, a, b), jnp.where(core == 0, b, a)], axis=1)

        proj_mine = lax.dynamic_slice_in_dim(proj, core * mine, mine, 0)
        proj_oth = partner(lax.dynamic_slice_in_dim(proj, (1 - core) * mine, mine, 0))
        stream = lat + own_first(proj_mine + proj_oth)
        squares = jnp.mean(stream * stream, axis=1, keepdims=True)
        normed = (stream * lax.rsqrt(squares + 1e-06) * gain).astype(BF)

        def ffn(x):
            pre = jnp.dot(x[:, :fh], up_proj, preferred_element_type=F32) + jnp.dot(
                x[:, fh:], up_oth, preferred_element_type=F32
            )
            hid = jax.nn.gelu(pre).astype(BF)
            return jnp.concatenate(
                [
                    jnp.dot(hid, down_proj, preferred_element_type=F32),
                    jnp.dot(hid, down_oth, preferred_element_type=F32),
                ],
                axis=1,
            )

        hm = mine // 2
        from_l, from_r = normed, normed
        outs = {}
        own = ffn(normed)
        for s in range(1, half):
            from_l, from_r = right(from_l), left(from_r)
            y = ffn(jnp.concatenate([from_l, from_r], axis=0))
            outs[-s], outs[s] = y[:mine], y[mine:]
        last_l, last_r = right(from_l[:hm]), left(from_r[hm:])
        far = ffn(jnp.concatenate([last_l, last_r], axis=0)).astype(BF)

        msg_r, msg_l = right(far[:hm]), left(far[hm:])
        for t in range(2, half + 1):
            a, b = outs[half - t + 1], outs[t - 1 - half]
            if t == 2:
                a = jnp.concatenate([a[:hm] + msg_r.astype(F32), a[hm:]], axis=0)
                b = jnp.concatenate([b[:hm], b[hm:] + msg_l.astype(F32)], axis=0)
            else:
                a, b = a + msg_r.astype(F32), b + msg_l.astype(F32)
            msg_r, msg_l = right(a.astype(BF)), left(b.astype(BF))
        total = stream + own + msg_r.astype(F32) + msg_l.astype(F32)
        total = total.astype(BF)
        keep, give = total[:, :fh], partner(total[:, fh:])
        return jnp.where(
            core == 0,
            jnp.concatenate([keep, give], axis=0),
            jnp.concatenate([give, keep], axis=0),
        )

    return shards


def solution(mesh):
    return jax.shard_map(
        make_shards(mesh.shape["hits"]),
        mesh=mesh,
        in_specs=(
            P("groups", "heads"),
            P(("groups", "hits"), "heads"),
            P(("groups", "hits"), "heads"),
            P(("groups", "hits")),
            P(("groups", "hits"), "heads"),
            P("heads", None),
            P("heads"),
            P("heads", "hits"),
            P("hits", "heads"),
        ),
        out_specs=P(("groups", "hits"), "heads"),
        check_vma=False,
    )
```

```python
import functools
import math

import jax
import jax.numpy as jnp
from jax import lax
from jax.experimental import pallas as pl
from jax.experimental.pallas import tpu as pltpu
from jax.sharding import PartitionSpec as P

HD = 128
BF = jnp.bfloat16
F32 = jnp.float32
EXP_SCALE = math.log2(math.e) / math.sqrt(HD)
DEAD = -1e30


def turned(x):
    k, rows = x.shape
    if k < HD:
        x = jnp.concatenate([x, jnp.zeros((HD - k, rows), x.dtype)], axis=0)
    return jnp.transpose(x)


VMEM_LIMIT = 16 * 2**20
vmem = pl.BlockSpec(memory_space=pltpu.VMEM)
smem = pl.BlockSpec(memory_space=pltpu.SMEM)


def local_call(kernel, out_shape, in_specs, name, flops, nbytes, exps=0, scratch=()):
    return pl.pallas_call(
        kernel,
        out_shape=[pltpu.VMEM(s.shape, s.dtype) for s in out_shape],
        in_specs=in_specs,
        out_specs=[vmem] * len(out_shape),
        scratch_shapes=list(scratch),
        cost_estimate=pl.CostEstimate(flops=flops, bytes_accessed=nbytes, transcendentals=exps),
        compiler_params=pltpu.CompilerParams(vmem_limit_bytes=VMEM_LIMIT),
        name=name,
    )


def attn_kernel(heads, blocks, rows, idx_ref, cnt_ref, q_ref, k_ref, v_ref, ctx_ref, st_ref, qs, sem):
    hits = k_ref.shape[0]
    copies = [
        pltpu.make_async_copy(
            q_ref.at[pl.ds(pl.multiple_of(idx_ref[b] * rows, rows), rows), :],
            qs.at[pl.ds(b * rows, rows), :],
            sem.at[b],
        )
        for b in range(blocks)
    ]
    for c in copies:
        c.start()
    live = lax.broadcasted_iota(jnp.int32, (1, hits), 1) < cnt_ref[0]
    bias = jnp.where(live, 0.0, DEAD)
    ones_v = jnp.ones((hits, HD), BF)
    lane = lax.broadcasted_iota(jnp.int32, (blocks * rows, HD), 1)
    for c in copies:
        c.wait()

    def scores(h):
        cols = slice(h * HD, (h + 1) * HD)
        s = lax.dot_general(
            qs[:, cols], k_ref[:, cols], (((1,), (1,)), ((), ())), preferred_element_type=F32
        )
        return s + bias

    st = jnp.zeros((blocks * rows, HD), F32)
    ahead = scores(0)
    for h in range(heads):
        s = ahead
        if h + 1 < heads:
            ahead = scores(h + 1)
        top = jnp.max(s, axis=1, keepdims=True).astype(BF).astype(F32)
        p = jnp.exp2((s - top) * EXP_SCALE).astype(BF)
        o = jnp.dot(
            p,
            jnp.concatenate([v_ref[:, h * HD : (h + 1) * HD], ones_v], axis=1),
            preferred_element_type=F32,
        )
        for b in range(blocks):
            at = (b * heads + h) * rows
            ctx_ref[at : at + rows, :] = o[b * rows : (b + 1) * rows, :HD]
        st = jnp.where(lane == h, top, st)
        st = jnp.where(lane == heads + h, o[:, HD:], st)
    st_ref[...] = jnp.transpose(st)[: 2 * heads]


def attend(idx, cnt, q, k, v, rows):
    blocks = idx.shape[0]
    hits, width = k.shape
    heads = width // HD
    n = blocks * rows
    return local_call(
        functools.partial(attn_kernel, heads, blocks, rows),
        [jax.ShapeDtypeStruct((n * heads, HD), F32), jax.ShapeDtypeStruct((2 * heads, n), F32)],
        [smem, smem, pl.BlockSpec(memory_space=pl.ANY), vmem, vmem],
        "attend",
        4 * n * hits * width,
        n * width * 6,
        n * hits * heads,
        [pltpu.VMEM((n, width), BF), pltpu.SemaphoreType.DMA((blocks,))],
    )(idx, cnt, q, k, v)


def group_rows(gh, rows):
    return gh * rows + 4 * gh


def read_group(msg_ref, base, gh, rows):
    st = msg_ref[base + gh * rows : base + gh * rows + 4 * gh, :rows].astype(F32)
    return st[:gh], st[gh : 2 * gh] + st[2 * gh : 3 * gh]


def write_stats(out_ref, base, gh, rows, top, total):
    hi = total.astype(BF).astype(F32)
    st = jnp.concatenate([top, hi, total - hi, jnp.zeros_like(top)], axis=0).astype(BF)
    if rows < HD:
        st = jnp.concatenate([st, jnp.zeros((4 * gh, HD - rows), BF)], axis=1)
    out_ref[base + gh * rows : base + gh * rows + 4 * gh, :] = st


def merge_kernel(heads, jobs, rows, *refs):
    gh = heads // 2
    gr = group_rows(gh, rows)
    ctx_ref, st_ref = refs[0], refs[1]
    n_msg = sum(1 for j in jobs if j[2])
    msgs, outs = refs[2 : 2 + n_msg], refs[2 + n_msg :]
    at = 0
    for (b, groups, held), out_ref in zip(jobs, outs):
        cols = slice(b * rows, (b + 1) * rows)
        msg_ref = None
        if held:
            msg_ref = msgs[at]
            at += 1
        for g in groups:
            base = groups.index(g) * gr
            own = (b * heads + g * gh) * rows
            top = st_ref[g * gh : (g + 1) * gh, cols]
            total = st_ref[heads + g * gh : heads + (g + 1) * gh, cols]
            if g in held:
                mbase = held.index(g) * gr
                mtop, mtotal = read_group(msg_ref, mbase, gh, rows)
                best = jnp.maximum(top, mtop)
                fa = jnp.exp2((top - best) * EXP_SCALE)
                fb = jnp.exp2((mtop - best) * EXP_SCALE)
                f = turned(jnp.concatenate([fa, fb], axis=0))
                for h in range(gh):
                    out_ref[base + h * rows : base + (h + 1) * rows, :] = (
                        ctx_ref[own + h * rows : own + (h + 1) * rows, :] * f[:, h : h + 1]
                        + msg_ref[mbase + h * rows : mbase + (h + 1) * rows, :].astype(F32)
                        * f[:, gh + h : gh + h + 1]
                    ).astype(BF)
                write_stats(out_ref, base, gh, rows, best, total * fa + mtotal * fb)
            else:
                out_ref[base : base + gh * rows, :] = ctx_ref[own : own + gh * rows, :].astype(BF)
                write_stats(out_ref, base, gh, rows, top, total)


def merge(ctx, st, msgs, jobs, heads, rows):
    gr = group_rows(heads // 2, rows)
    outs = [jax.ShapeDtypeStruct((len(j[1]) * gr, HD), BF) for j in jobs]
    nbytes = sum(len(j[1]) * gr * HD * 8 for j in jobs)
    return local_call(
        functools.partial(merge_kernel, heads, jobs, rows),
        outs,
        [vmem] * (2 + len(msgs)),
        "merge",
        nbytes,
        nbytes,
    )(ctx, st, *msgs)


def project_kernel(heads, rows, core_ref, ctx_ref, st_ref, a_ref, b_ref, w_ref, mine_ref, theirs_ref, ctx_s):
    gh = heads // 2
    gr = group_rows(gh, rows)
    for g in range(2):
        top = st_ref[g * gh : (g + 1) * gh, :]
        total = st_ref[heads + g * gh : heads + (g + 1) * gh, :]
        atop, atotal = read_group(a_ref, g * gr, gh, rows)
        btop, btotal = read_group(b_ref, g * gr, gh, rows)
        best = jnp.maximum(jnp.maximum(top, atop), btop)
        f0 = jnp.exp2((top - best) * EXP_SCALE)
        fa = jnp.exp2((atop - best) * EXP_SCALE)
        fb = jnp.exp2((btop - best) * EXP_SCALE)
        total = total * f0 + atotal * fa + btotal * fb
        f = turned(jnp.concatenate([f0 / total, fa / total, fb / total], axis=0))
        for h in range(gh):
            own = slice((g * gh + h) * rows, (g * gh + h + 1) * rows)
            far = slice(g * gr + h * rows, g * gr + (h + 1) * rows)
            ctx_s[:, (g * gh + h) * HD : (g * gh + h + 1) * HD] = (
                ctx_ref[own, :] * f[:, h : h + 1]
                + a_ref[far, :].astype(F32) * f[:, gh + h : gh + h + 1]
                + b_ref[far, :].astype(F32) * f[:, 2 * gh + h : 2 * gh + h + 1]
            ).astype(BF)
    mine, fh = rows // 2, w_ref.shape[1] // 2
    core = core_ref[0]
    keep = pl.ds(pl.multiple_of(core * mine, mine), mine)
    give = pl.ds(pl.multiple_of((1 - core) * mine, mine), mine)
    near = pl.ds(pl.multiple_of(core * fh, fh), fh)
    away = pl.ds(pl.multiple_of((1 - core) * fh, fh), fh)
    both = jnp.concatenate([ctx_s[keep, :], ctx_s[give, :]], axis=0)
    for cols, here, there in ((near, 0, 1), (away, 1, 0)):
        y = jnp.dot(both, w_ref[:, cols], preferred_element_type=F32)
        mine_ref[:, here * fh : (here + 1) * fh] = y[:mine]
        theirs_ref[:, there * fh : (there + 1) * fh] = y[mine:]


def project(core, ctx, st, a, b, w, heads, rows):
    out = jax.ShapeDtypeStruct((rows // 2, w.shape[1]), F32)
    return local_call(
        functools.partial(project_kernel, heads, rows),
        [out, out],
        [smem] + [vmem] * 5,
        "project",
        2 * rows * w.size,
        rows * heads * HD * 10 + w.size * 2,
        0,
        [pltpu.VMEM((rows, heads * HD), BF)],
    )(core, ctx, st, a, b, w)


def norm_kernel(mine_ref, theirs_ref, la_ref, lb_ref, ga_ref, gb_ref, stream_ref, normed_ref):
    fh = la_ref.shape[1]
    x = [
        mine_ref[:, c] + theirs_ref[:, c] + l[...].astype(F32)
        for c, l in ((slice(0, fh), la_ref), (slice(fh, 2 * fh), lb_ref))
    ]
    squares = sum(jnp.sum(v * v, axis=1, keepdims=True) for v in x) / (2 * fh)
    scale = lax.rsqrt(squares + 1e-06)
    for i, g in enumerate((ga_ref, gb_ref)):
        stream_ref[:, i * fh : (i + 1) * fh] = x[i]
        normed_ref[:, i * fh : (i + 1) * fh] = (x[i] * scale * g[...]).astype(BF)


def ffn_kernel(m, *refs):
    xs, (ua, ub, da, db), outs = refs[:m], refs[m : m + 4], refs[m + 4 :]
    fh = ua.shape[0]
    x = xs[0][...] if m == 1 else jnp.concatenate([r[...] for r in xs], axis=0)
    pre = jnp.dot(x[:, :fh], ua[...], preferred_element_type=F32)
    pre += jnp.dot(x[:, fh:], ub[...], preferred_element_type=F32)
    hid = jax.nn.gelu(pre).astype(BF)
    for i, w in enumerate((da, db)):
        y = jnp.dot(hid, w[...], preferred_element_type=F32)
        at = 0
        for r, o in zip(xs, outs):
            o[:, i * fh : (i + 1) * fh] = y[at : at + r.shape[0]].astype(o.dtype)
            at += r.shape[0]


def ffn(xs, weights, dtype):
    size = sum(w.size for w in weights)
    m = sum(x.shape[0] for x in xs)
    return local_call(
        functools.partial(ffn_kernel, len(xs)),
        [jax.ShapeDtypeStruct(x.shape, dtype) for x in xs],
        [vmem] * (len(xs) + 4),
        "ffn",
        2 * m * size,
        2 * size,
        m * weights[0].shape[1],
    )(*xs, *weights)


def make_shards(n):
    half = n // 2
    order = list(range(0, n, 2)) + list(range(n - 1, 0, -2))
    fwd = [(order[i], order[(i + 1) % n]) for i in range(n)]
    bwd = [(b, a) for a, b in fwd]
    swap = [(0, 1), (1, 0)]

    right = lambda x: lax.ppermute(x, "hits", fwd)
    left = lambda x: lax.ppermute(x, "hits", bwd)
    partner = lambda x: lax.ppermute(x, "heads", swap)

    def shards(queries, keys, values, hit_counts, latents, out_proj, norm_gain, up_proj, down_proj):
        core = lax.axis_index("heads")
        me = lax.axis_index("hits")
        pos = jnp.where(me % 2 == 0, me // 2, n - 1 - me // 2)

        def block_at(k):
            p = lax.rem(pos + (k + n), n)
            return jnp.where(p < half, 2 * p, 2 * (n - 1 - p) + 1)

        rows = latents.shape[0]
        mine = rows // 2
        width = keys.shape[1]
        heads = width // HD
        feats = 2 * latents.shape[1]
        fh = latents.shape[1]
        cnt = hit_counts.astype(jnp.int32)

        up_oth = partner(up_proj)
        down_oth = partner(down_proj)
        gain_own = norm_gain.reshape(1, fh)
        gain_oth = partner(gain_own)
        lat_own = lax.dynamic_slice_in_dim(latents, core * mine, mine, 0)
        lat_oth = partner(lax.dynamic_slice_in_dim(latents, (1 - core) * mine, mine, 0))

        def partial(ks):
            idx = jnp.stack([block_at(k) for k in ks]).astype(jnp.int32)
            return attend(idx, cnt, queries, keys, values, rows)

        ctx, st = partial([half])
        msg_r, msg_l = merge(ctx, st, [], ((0, (0,), ()), (0, (1,), ())), heads, rows)
        held_r, held_l = (0,), (1,)
        for t in range(2, half + 1):
            msg_r, msg_l = right(msg_r), left(msg_l)
            ctx, st = partial([half - t + 1, t - 1 - half])
            msg_r, msg_l = merge(
                ctx, st, [msg_r, msg_l], ((0, (0, 1), held_r), (1, (0, 1), held_l)), heads, rows
            )
            held_r = held_l = (0, 1)
        msg_r, msg_l = right(msg_r), left(msg_l)
        ctx, st = partial([0])
        core_id = core.reshape(1).astype(jnp.int32)
        proj, proj_oth = project(core_id, ctx, st, msg_r, msg_l, out_proj, heads, rows)
        proj_oth = partner(proj_oth)
        stream, normed = local_call(
            norm_kernel,
            [jax.ShapeDtypeStruct((mine, feats), F32), jax.ShapeDtypeStruct((mine, feats), BF)],
            [vmem] * 6,
            "norm",
            mine * feats * 8,
            mine * feats * 18,
        )(proj, proj_oth, lat_own, lat_oth, gain_own, gain_oth)
        weights = (up_proj, up_oth, down_proj, down_oth)

        hm = mine // 2
        from_l, from_r = normed, normed
        outs = {}
        for s in range(1, half):
            from_l, from_r = right(from_l), left(from_r)
            outs[-s], outs[s] = ffn([from_l, from_r], weights, F32)
        last_l, last_r = right(from_l[:hm]), left(from_r[hm:])
        far_r, far_l = ffn([last_l, last_r], weights, BF)
        own = ffn([normed], weights, F32)[0]

        msg_r, msg_l = right(far_r), left(far_l)
        for t in range(2, half + 1):
            a, b = outs[half - t + 1], outs[t - 1 - half]
            if t == 2:
                a = jnp.concatenate([a[:hm] + msg_r.astype(F32), a[hm:]], axis=0)
                b = jnp.concatenate([b[:hm], b[hm:] + msg_l.astype(F32)], axis=0)
            else:
                a, b = a + msg_r.astype(F32), b + msg_l.astype(F32)
            msg_r, msg_l = right(a.astype(BF)), left(b.astype(BF))
        total = stream + own + msg_r.astype(F32) + msg_l.astype(F32)
        total = total.astype(BF)
        keep, give = total[:, :fh], partner(total[:, fh:])
        return jnp.where(
            core == 0,
            jnp.concatenate([keep, give], axis=0),
            jnp.concatenate([give, keep], axis=0),
        )

    return shards


def solution(mesh):
    return jax.shard_map(
        make_shards(mesh.shape["hits"]),
        mesh=mesh,
        in_specs=(
            P("groups", "heads"),
            P(("groups", "hits"), "heads"),
            P(("groups", "hits"), "heads"),
            P(("groups", "hits")),
            P(("groups", "hits"), "heads"),
            P("heads", None),
            P("heads"),
            P("heads", "hits"),
            P("hits", "heads"),
        ),
        out_specs=P(("groups", "hits"), "heads"),
        check_vma=False,
    )
```
